32 devices in a mesh: lon: 8 (over z, core), lat: 4 (over y, x).
Axes of the slice: x: 2, y: 2, z: 4, core: 2. Of those that a mesh axis runs over, the one named last changes fastest.
Arguments:
- tracers: float32 [32, 32, 16384], P(None, 'lat', 'lon'), may hold values from 0.1 to 10
- courant: float32 [2, 32, 256], P(None, 'lat', 'lon'), may hold values from -0.45 to 0.45
- switches: int32 [2, 32, 256], P(None, 'lat', 'lon'), may hold values 0 or 1
- day_flags: int32 [32, 256], P('lat', 'lon'), may hold values from 0 to 1, as said below
- diffusion_counts: int32 [32, 256], P('lat', 'lon'), may hold values from 1 to 8
- night_rates: float32 [32, 32], replicated, may hold values from -0.18 to 0.18
- photo_rates: float32 [32, 32], replicated, may hold values from -0.24 to 0.24
- level_light: float32 [64], replicated, may hold values from 0.1 to 1
- self_loss: float32 [32], replicated, may hold values from 0.001 to 0.05
- vertical_mixing: float32 [63], replicated, may hold values from 0.05 to 0.45
Outputs:
- tracers_out: float32 [32, 32, 16384], P(None, 'lat', 'lon')
The draws below stay inside these ranges and needn't reach their ends.
Inputs may be any that keep to these rules, and one draw needn't show every extreme that they name: `day_flags`: in every latitude row exactly half of the 256 columns are day columns, forming one contiguous band around the longitude cycle.
All inputs are finite; a program needn't handle non-finite values. No bound on the sum of `switches` on one device may be relied on, other than what follows from the above.
Results may differ from the reference program's by a relative error of at most 0.0003.
Values sent between devices are 32-bit elements; how exact they have to be, the bound alone decides.
A program may use at most 64 MiB of HBM per device.

```python
import math
import jax
import jax.numpy as jnp
from jax import lax

SPECIES = 32
LEVELS = 64
CHEM = 6
KMAX = 8
NLAT = 32
NLON = 256


def column_plan(key):
    base_key = jax.random.fold_in(key, 4099)
    key_offset, key_jitter, key_night, key_day = jax.random.split(base_key, 4)
    offset = jax.random.randint(key_offset, (), 0, NLON)
    jitter = jax.random.randint(key_jitter, (NLAT, 1), -2, 3)
    longitude = jnp.arange(NLON, dtype=jnp.int32)[None, :]
    daylight = ((longitude - offset - jitter) % NLON < NLON // 2).astype(jnp.int32)
    night_counts = jax.random.randint(key_night, (NLAT, NLON), 1, KMAX // 2 + 1)
    day_counts = jax.random.randint(key_day, (NLAT, NLON), KMAX // 2, KMAX + 1)
    substeps = jnp.where(daylight == 1, day_counts, night_counts).astype(jnp.int32)
    substeps = substeps.at[0, 0].set(KMAX).at[NLAT - 1, NLON - 1].set(1)
    return (daylight, substeps)


def draw_day_flags(key, part):
    return column_plan(key)[0]


def draw_diffusion_counts(key, part):
    return column_plan(key)[1]


def set_ends(values, stream_key, low, top_value):
    index_at = [jax.random.randint(jax.random.fold_in(stream_key, axis), (), 0, length) for axis, length in enumerate(values.shape)]
    main_axis = values.shape.index(max(values.shape))
    next_to = index_at[:main_axis] + [(index_at[main_axis] + 1) % values.shape[main_axis]] + index_at[main_axis + 1:]
    return values.at[tuple(index_at)].set(low).at[tuple(next_to)].set(top_value)


def block_scale(rng, dims, cuts, smallest, top_value):
    def one(position, blocks):
        heights = jax.random.uniform(jax.random.fold_in(jax.random.fold_in(rng, 6), position), (blocks,), jnp.float32, smallest / len(cuts), top_value / len(cuts))
        return jnp.repeat(jnp.exp(heights), dims[position] // blocks).reshape((-1,) + (1,) * (len(dims) - position - 1))

    factor_of = one(*cuts[0])
    for cut in cuts[1:]:
        factor_of = factor_of * one(*cut)
    return factor_of


def bell_draw(key, shape, spread, most, held_as=jnp.bfloat16):
    entries = jax.random.normal(key, shape, jnp.float32) * spread
    return jnp.minimum(jnp.maximum(entries, -most), most).astype(held_as)


def setup_inputs(seed: int = 0) -> dict:
    streams_of = jax.random.split(jax.random.key(seed), 11)
    return {
        "tracers": jnp.clip(jnp.exp(math.log(10.0) - 4.6051702 * jax.random.uniform(streams_of[0], (SPECIES, NLAT, NLON * LEVELS), jnp.float32) ** block_scale(streams_of[0], (SPECIES, NLAT, NLON * LEVELS), ((1, 4), (2, 8)), -0.2, 0.2)), 0.1, 10.0),
        "courant": jnp.clip(jax.random.uniform(streams_of[1], (2, NLAT, NLON), jnp.float32, -0.45, 0.45) * block_scale(streams_of[1], (2, NLAT, NLON), ((1, 4), (2, 8)), -0.4, 0.0), -0.45, 0.45),
        "switches": set_ends((jax.random.randint(streams_of[2], (2, NLAT, NLON), 0, 4) < 3).astype(jnp.int32), jax.random.fold_in(streams_of[2], 1), 0, 1),
        "day_flags": draw_day_flags(jax.random.fold_in(streams_of[10], 71), 0),
        "diffusion_counts": draw_diffusion_counts(jax.random.fold_in(streams_of[10], 71), 0),
        "night_rates": bell_draw(streams_of[5], (SPECIES, SPECIES), 0.03, 0.18, jnp.float32),
        "photo_rates": bell_draw(streams_of[6], (SPECIES, SPECIES), 0.04, 0.24, jnp.float32),
        "level_light": jnp.clip(jnp.exp(jax.random.uniform(streams_of[7], (LEVELS,), jnp.float32, math.log(0.1), math.log(1.0))), 0.1, 1.0),
        "self_loss": jnp.clip(jnp.exp(jax.random.uniform(streams_of[8], (SPECIES,), jnp.float32, math.log(0.001), math.log(0.05))), 0.001, 0.05),
        "vertical_mixing": jnp.clip(jax.random.uniform(streams_of[9], (LEVELS - 1,), jnp.float32, 0.05, 0.45), 0.05, 0.45),
    }


def minmod(left, right):
    return 0.5 * (jnp.sign(left) + jnp.sign(right)) * jnp.minimum(jnp.abs(left), jnp.abs(right))


def advect_sweep(extended, cour, switch, along_axis, cell_count, cell_unit):
    def take_cells(first_cell, number):
        return lax.slice_in_dim(extended, first_cell * cell_unit, (first_cell + number) * cell_unit, axis=along_axis)

    second_left = take_cells(0, cell_count + 1)
    first_left = take_cells(1, cell_count + 1)
    first_right = take_cells(2, cell_count + 1)
    second_right = take_cells(3, cell_count + 1)
    plus_flux = cour * (first_left + 0.5 * (1.0 - cour) * switch * minmod(first_left - second_left, first_right - first_left))
    minus_flux = cour * (first_right - 0.5 * (1.0 + cour) * switch * minmod(first_right - first_left, second_right - first_right))
    face_flux = jnp.where(cour >= 0.0, plus_flux, minus_flux)
    upper_faces = lax.slice_in_dim(face_flux, cell_unit, (cell_count + 1) * cell_unit, axis=along_axis)
    lower_faces = lax.slice_in_dim(face_flux, 0, cell_count * cell_unit, axis=along_axis)
    return take_cells(2, cell_count) - (upper_faces - lower_faces)


def react_mix(tracer_block, daylight, substeps, rate_rows, level_light, self_loss, vertical_mixing, loop_count):
    species = tracer_block.shape[0]
    levels = level_light.shape[0]
    column = daylight.shape[-1]
    sunlight = jnp.repeat(daylight.astype(jnp.float32), levels, axis=-1) * jnp.tile(level_light, column)
    self_term = self_loss.reshape((species,) + (1,) * (tracer_block.ndim - 1))
    for _ in range(CHEM):
        flat = tracer_block.reshape(species, -1)
        joined = jnp.dot(rate_rows, flat, precision=lax.Precision.HIGHEST).reshape((2,) + tracer_block.shape)
        tracer_block = (tracer_block + joined[0] + sunlight * joined[1]) / (1.0 + self_term * tracer_block * tracer_block)
    mixing_faces = jnp.tile(jnp.concatenate([vertical_mixing, jnp.zeros((1,), vertical_mixing.dtype)]), column)
    step_limits = jnp.repeat(substeps, levels, axis=-1)

    def mix_step(step_index, tracer_field):
        edge = jnp.zeros_like(tracer_field[..., :1])
        above_cells = jnp.concatenate([tracer_field[..., 1:], edge], -1)
        level_flux = mixing_faces * (above_cells - tracer_field)
        below_flux = jnp.concatenate([edge, level_flux[..., :-1]], -1)
        return jnp.where(step_index < step_limits, tracer_field + level_flux - below_flux, tracer_field)

    return lax.fori_loop(0, loop_count, mix_step, tracer_block)


def reference(tracers, courant, switches, day_flags, diffusion_counts, night_rates, photo_rates, level_light, self_loss, vertical_mixing):
    switch_float = switches.astype(jnp.float32)
    lon_cour = jnp.concatenate([courant[0], courant[0][:, :1]], 1)
    lon_switch = jnp.concatenate([switch_float[0], switch_float[0][:, :1]], 1)
    row_valid = (jnp.arange(NLAT) >= 1).astype(jnp.float32)[:, None]
    lat_cour = jnp.concatenate([courant[1] * row_valid, jnp.zeros((1, NLON), jnp.float32)], 0)
    lat_switch = jnp.concatenate([switch_float[1], jnp.zeros((1, NLON), jnp.float32)], 0)
    lon_cour = jnp.repeat(lon_cour, LEVELS, axis=1)
    lon_switch = jnp.repeat(lon_switch, LEVELS, axis=1)
    lat_cour = jnp.repeat(lat_cour, LEVELS, axis=1)
    lat_switch = jnp.repeat(lat_switch, LEVELS, axis=1)

    def transport(tracer_field):
        extended = jnp.concatenate([tracer_field[:, -2 * LEVELS:], tracer_field, tracer_field[:, :2 * LEVELS]], 1)
        midway = advect_sweep(extended, lon_cour, lon_switch, 1, NLON, LEVELS)
        extended = jnp.pad(midway, ((2, 2), (0, 0)))
        return advect_sweep(extended, lat_cour, lat_switch, 0, NLAT, 1)

    rate_rows = jnp.concatenate([night_rates, photo_rates], 0)
    advected = lax.map(transport, tracers)

    def column_work(item):
        tracer_block, daylight, substeps = item
        return react_mix(tracer_block, daylight, substeps, rate_rows, level_light, self_loss, vertical_mixing, KMAX)

    reacted = lax.map(column_work, (jnp.moveaxis(advected, 1, 0), day_flags, diffusion_counts))
    return lax.map(transport, jnp.moveaxis(reacted, 0, 1))
```

```python
import functools

import jax
import jax.numpy as jnp
from jax import lax
from jax.experimental import pallas as pl
from jax.experimental.pallas import tpu as pltpu
from jax.sharding import PartitionSpec as P

CHEM = 6
KMAX = 8
WIDE = 512
MESH = pl.DeviceIdType.MESH


def minmod(x, y):
    return jnp.maximum(jnp.minimum(x, y), 0.0) + jnp.minimum(jnp.maximum(x, y), 0.0)


def face_flux(c, coef, aa, a, b, bb):
    pos = c >= 0.0
    x = jnp.where(pos, a - aa, bb - b)
    return c * (jnp.where(pos, a, b) + coef * minmod(x, b - a))


def kernel(
    unit,
    x_ref,
    lonc_ref,
    lonk_ref,
    latc_ref,
    latk_ref,
    sun_ref,
    cnt_ref,
    mix_ref,
    w_ref,
    loss_ref,
    out_ref,
    mid_ref,
    state_ref,
    again_ref,
    west_ref,
    east_ref,
    south_ref,
    north_ref,
    lon_send,
    lon_recv,
    lat_send,
    lat_recv,
):
    rows, species, lanes = x_ref.shape
    tiles = lanes // unit
    edge = 2
    nlon, nlat = lax.axis_size("lon"), lax.axis_size("lat")
    lon, lat = lax.axis_index("lon"), lax.axis_index("lat")
    east, west = lax.rem(lon + 1, nlon), lax.rem(lon + nlon - 1, nlon)
    has_south, has_north = lat > 0, lat < nlat - 1

    barrier = pltpu.get_barrier_semaphore()
    for side in (east, west):
        pl.semaphore_signal(barrier, inc=1, device_id={"lon": side}, device_id_type=MESH)

    @pl.when(has_south)
    def _():
        pl.semaphore_signal(barrier, inc=1, device_id={"lat": lat - 1}, device_id_type=MESH)

    @pl.when(has_north)
    def _():
        pl.semaphore_signal(barrier, inc=1, device_id={"lat": lat + 1}, device_id_type=MESH)

    @pl.when(jnp.logical_not(has_south))
    def _():
        south_ref[...] = jnp.zeros_like(south_ref)
        pl.semaphore_wait(barrier, 3)

    @pl.when(jnp.logical_not(has_north))
    def _():
        north_ref[...] = jnp.zeros_like(north_ref)
        pl.semaphore_wait(barrier, 3)

    @pl.when(jnp.logical_and(has_south, has_north))
    def _():
        pl.semaphore_wait(barrier, 4)

    groups = ((0, edge), (rows - edge, edge), (edge, rows - 2 * edge))

    def lon_copies(source, turn, group):
        first, number = groups[group]
        held = pl.ds(first, number)
        pairs = (
            (source.at[held, :, pl.ds(lanes - unit, unit)], west_ref.at[turn, held], east),
            (source.at[held, :, pl.ds(0, unit)], east_ref.at[turn, held], west),
        )
        return [
            pltpu.make_async_remote_copy(
                src_ref=src,
                dst_ref=dst,
                send_sem=lon_send.at[turn, group, way],
                recv_sem=lon_recv.at[turn, group, way],
                device_id={"lon": to},
                device_id_type=MESH,
            )
            for way, (src, dst, to) in enumerate(pairs)
        ]

    def lat_copies(source, turn):
        up = pltpu.make_async_remote_copy(
            src_ref=source.at[pl.ds(rows - edge, edge)],
            dst_ref=south_ref.at[turn],
            send_sem=lat_send.at[turn, 0],
            recv_sem=lat_recv.at[turn, 0],
            device_id={"lat": lat + 1},
            device_id_type=MESH,
        )
        down = pltpu.make_async_remote_copy(
            src_ref=source.at[pl.ds(0, edge)],
            dst_ref=north_ref.at[turn],
            send_sem=lat_send.at[turn, 1],
            recv_sem=lat_recv.at[turn, 1],
            device_id={"lat": lat - 1},
            device_id_type=MESH,
        )
        return up, down

    def lat_start(source, turn):
        up, down = lat_copies(source, turn)

        @pl.when(has_north)
        def _():
            up.start()

        @pl.when(has_south)
        def _():
            down.start()

    def lat_wait(source, turn):
        up, down = lat_copies(source, turn)

        @pl.when(has_north)
        def _():
            up.wait_send()
            down.wait_recv()

        @pl.when(has_south)
        def _():
            down.wait_send()
            up.wait_recv()

    def edge_row(i):
        return i + (i // edge) * (rows - 2 * edge)

    low = lax.broadcasted_iota(jnp.int32, (species, unit), 1) < unit // 2

    def lon_sweep(source, target, turn, number, row_of):
        def one(i, carry):
            row = row_of(i)

            def tile(j):
                if j < 0:
                    return west_ref[turn, row]
                if j == tiles:
                    return east_ref[turn, row]
                return source[row, :, j * unit : (j + 1) * unit]

            def swap(v):
                return pltpu.roll(v, unit // 2, 1)

            before, here = tile(-1), tile(0)
            swapped = swap(here)
            behind = jnp.where(low, swap(before), swapped)
            flux, turned, cell = None, None, None
            for j in range(tiles + 1):
                if j < tiles:
                    after = tile(j + 1)
                    after_swapped = swap(after)
                    ahead = jnp.where(low, swapped, after_swapped)
                else:
                    after, after_swapped, ahead = here, swapped, swapped
                at = slice(j * unit, (j + 1) * unit)
                c = lonc_ref[row, :, at]
                k = lonk_ref[row, :, at]
                now = face_flux(c, k, before, behind, here, ahead)
                now_turned = swap(now)
                if j > 0:
                    upper = jnp.where(low, turned, now_turned)
                    target[row, :, (j - 1) * unit : j * unit] = cell - (upper - flux)
                flux, turned, cell = now, now_turned, here
                before, here, behind, swapped = here, after, ahead, after_swapped
            return carry

        lax.fori_loop(0, number, one, 0)

    def lat_sweep(source, target, turn, spans):
        def one(j, carry):
            at = pl.ds(pl.multiple_of(j * unit, unit), unit)

            def cell(row):
                if row < 0:
                    return south_ref[turn, row + edge, :, at]
                if row >= rows:
                    return north_ref[turn, row - rows, :, at]
                return source[row, :, at]

            for first, last in spans:
                aa, a, b = cell(first - 2), cell(first - 1), cell(first)
                flux = None
                for row in range(first, last + 1):
                    bb = cell(row + 1)
                    c = latc_ref[row, :, at]
                    k = latk_ref[row, :, at]
                    now = face_flux(c, k, aa, a, b, bb)
                    if flux is not None:
                        target[row - 1, :, at] = a - (now - flux)
                    flux = now
                    aa, a, b = a, b, bb
            return carry

        lax.fori_loop(0, tiles, one, 0)

    wide = min(WIDE, lanes)
    pieces = lanes // wide

    def chemistry(number, row_of):
        def one(i, carry):
            row = row_of(i // pieces)
            start = pl.multiple_of((i % pieces) * wide, wide)
            at = pl.ds(start, wide)
            q = state_ref[row, :, at]
            sun = sun_ref[row, :, at]
            loss = loss_ref[...]
            for _ in range(CHEM):
                high = q.astype(jnp.bfloat16)
                rest = (q - high.astype(jnp.float32)).astype(jnp.bfloat16)
                both = jnp.dot(
                    w_ref[...],
                    jnp.concatenate([high, rest, high], 0),
                    preferred_element_type=jnp.float32,
                )
                q = (q + both[:species] + sun * both[species:]) / (1.0 + loss * q * q)
            for t in range(wide // unit):
                v = q[:, t * unit : (t + 1) * unit]
                here = pl.ds(start + t * unit, unit)
                count = cnt_ref[row, :, here]
                for step in range(KMAX):
                    m = jnp.where(step < count, mix_ref[...], 0.0)
                    flow = m * (pltpu.roll(v, unit - 1, 1) - v)
                    v = v + flow - pltpu.roll(flow, 1, 1)
                state_ref[row, :, here] = v
            return carry

        lax.fori_loop(0, number * pieces, one, 0)

    inner = rows - 2 * edge
    edge_spans = ((0, edge), (rows - edge, rows))
    inner_spans = ((edge, rows - edge),)

    def inner_row(i):
        return i + edge

    first = [lon_copies(x_ref, 0, group) for group in range(3)]
    for pair in first:
        for copy in pair:
            copy.start()
    for pair in first[:2]:
        for copy in pair:
            copy.wait()
    lon_sweep(x_ref, mid_ref, 0, 2 * edge, edge_row)
    lat_start(mid_ref, 0)
    for copy in first[2]:
        copy.wait()
    lon_sweep(x_ref, mid_ref, 0, inner, inner_row)
    lat_sweep(mid_ref, state_ref, 0, inner_spans)
    chemistry(inner, inner_row)
    second = [lon_copies(state_ref, 1, group) for group in range(3)]
    for copy in second[2]:
        copy.start()
    lat_wait(mid_ref, 0)
    lat_sweep(mid_ref, state_ref, 0, edge_spans)
    chemistry(2 * edge, edge_row)
    for pair in second[:2]:
        for copy in pair:
            copy.start()
    for pair in second[:2]:
        for copy in pair:
            copy.wait()
    lon_sweep(state_ref, again_ref, 1, 2 * edge, edge_row)
    lat_start(again_ref, 1)
    for copy in second[2]:
        copy.wait()
    lon_sweep(state_ref, again_ref, 1, inner, inner_row)
    lat_sweep(again_ref, out_ref, 1, inner_spans)
    lat_wait(again_ref, 1)
    lat_sweep(again_ref, out_ref, 1, edge_spans)


def shifted(value, axis, steps):
    count = lax.axis_size(axis)
    return lax.ppermute(value, axis, [(i, (i + steps) % count) for i in range(count)])


def from_ahead(value, axis):
    count = lax.axis_size(axis)
    return lax.ppermute(value, axis, [(i + 1, i) for i in range(count - 1)])


def slopes(c, m):
    return jnp.where(c >= 0.0, 0.5 * (1.0 - c), -0.5 * (1.0 + c)) * m


def shards(
    tracers,
    courant,
    switches,
    day_flags,
    diffusion_counts,
    night_rates,
    photo_rates,
    level_light,
    self_loss,
    vertical_mixing,
):
    species, rows, lanes = tracers.shape
    levels = level_light.shape[0]
    columns = lanes // levels
    unit = 2 * levels
    f32 = jnp.float32
    nlat = lax.axis_size("lat")
    faces = jnp.concatenate([courant, switches.astype(f32)], 0)
    east_faces = shifted(faces[0::2, :, :1], "lon", -1)
    north_faces = from_ahead(faces[1::2, :1], "lat")
    lon_faces = jnp.concatenate([faces[0::2], east_faces, east_faces], 2)
    lat_faces = jnp.concatenate([faces[1::2], north_faces], 1)
    global_face = lax.axis_index("lat") * rows + jnp.arange(rows + 1, dtype=jnp.int32)
    valid = ((global_face >= 1) & (global_face < rows * nlat)).astype(f32)[:, None]
    lat_c = lat_faces[0] * valid
    spread = functools.partial(jnp.repeat, repeats=levels, axis=-1)
    lon_c = spread(lon_faces[0])
    lon_k = spread(slopes(lon_faces[0], lon_faces[1]))
    lat_k = spread(slopes(lat_c, lat_faces[1]))
    lat_c = spread(lat_c)
    sun = spread(day_flags.astype(f32)) * jnp.tile(level_light, columns)
    counts = spread(diffusion_counts)
    mixing = jnp.concatenate([vertical_mixing, jnp.zeros((1,), f32)])
    mixing = jnp.tile(mixing, 2)[None]
    rates = jnp.concatenate([night_rates, photo_rates], 0)
    top = lax.reduce_precision(rates, 8, 7)
    rest = (rates - top).astype(jnp.bfloat16)
    top = top.astype(jnp.bfloat16)
    weights = jnp.concatenate([top, top, rest], 1)
    block = (rows, species, lanes)
    out = pl.pallas_call(
        functools.partial(kernel, unit),
        out_shape=jax.ShapeDtypeStruct(block, f32),
        in_specs=[pl.BlockSpec(memory_space=pltpu.VMEM)] * 10,
        out_specs=pl.BlockSpec(memory_space=pltpu.VMEM),
        scratch_shapes=[
            pltpu.VMEM(block, f32),
            pltpu.VMEM(block, f32),
            pltpu.VMEM(block, f32),
            pltpu.VMEM((2, rows, species, unit), f32),
            pltpu.VMEM((2, rows, species, unit), f32),
            pltpu.VMEM((2, 2, species, lanes), f32),
            pltpu.VMEM((2, 2, species, lanes), f32),
            pltpu.SemaphoreType.DMA((2, 3, 2)),
            pltpu.SemaphoreType.DMA((2, 3, 2)),
            pltpu.SemaphoreType.DMA((2, 2)),
            pltpu.SemaphoreType.DMA((2, 2)),
        ],
        compiler_params=pltpu.CompilerParams(
            collective_id=0, has_side_effects=True, vmem_limit_bytes=48 * 1024 * 1024
        ),
    )(
        jnp.transpose(tracers, (1, 0, 2)),
        lon_c[:, None],
        lon_k[:, None],
        lat_c[:, None],
        lat_k[:, None],
        sun[:, None],
        counts[:, None],
        mixing,
        weights,
        self_loss[:, None],
    )
    return jnp.transpose(out, (1, 0, 2))


def solution(mesh):
    grid = P(None, "lat", "lon")
    plane = P("lat", "lon")
    in_specs = (grid, grid, grid, plane, plane, P(), P(), P(), P(), P())
    return jax.shard_map(shards, mesh=mesh, in_specs=in_specs, out_specs=grid, check_vma=False)
```

```python
import functools

import jax
import jax.numpy as jnp
from jax import lax
from jax.experimental import pallas as pl
from jax.experimental.pallas import tpu as pltpu
from jax.sharding import PartitionSpec as P

CHEM = 6
KMAX = 8
WIDE = 2048
MESH = pl.DeviceIdType.MESH


def minmod(x, y):
    return jnp.maximum(jnp.minimum(x, y), 0.0) + jnp.minimum(jnp.maximum(x, y), 0.0)


def face_flux(c, coef, aa, a, b, bb):
    pos = c >= 0.0
    x = jnp.where(pos, a - aa, bb - b)
    return c * (jnp.where(pos, a, b) + coef * minmod(x, b - a))


def build_powers(unit, mix_ref, power_ref):
    source = lax.broadcasted_iota(jnp.int32, (unit, unit), 0)
    target = lax.broadcasted_iota(jnp.int32, (unit, unit), 1)
    up = jnp.broadcast_to(mix_ref[...], (unit, unit))
    down = pltpu.roll(up, 1, 1)
    one = jnp.where(source == target, 1.0 - up - down, 0.0)
    one = jnp.where(source == target + 1, up, one)
    one = jnp.where(source == target - 1, down, one)
    powers = {1: one}
    for n in range(2, KMAX + 1):
        half = n // 2
        powers[n] = jnp.dot(
            powers[half],
            powers[n - half],
            precision=lax.Precision.HIGHEST,
            preferred_element_type=jnp.float32,
        )
    for n, power in powers.items():
        at = slice((n - 1) * unit, n * unit)
        top = power.astype(jnp.bfloat16)
        power_ref[:unit, at] = top
        power_ref[unit : 2 * unit, at] = top
        power_ref[2 * unit :, at] = (power - top.astype(jnp.float32)).astype(jnp.bfloat16)


def kernel(
    unit,
    x_ref,
    lonc_ref,
    lonk_ref,
    latc_ref,
    latk_ref,
    sun_ref,
    cnt_ref,
    mix_ref,
    w_ref,
    loss_ref,
    out_ref,
    mid_ref,
    state_ref,
    again_ref,
    west_ref,
    east_ref,
    south_ref,
    north_ref,
    power_ref,
    lon_send,
    lon_recv,
    lat_send,
    lat_recv,
):
    rows, species, lanes = x_ref.shape
    tiles = lanes // unit
    edge = 2
    nlon, nlat = lax.axis_size("lon"), lax.axis_size("lat")
    lon, lat = lax.axis_index("lon"), lax.axis_index("lat")
    east, west = lax.rem(lon + 1, nlon), lax.rem(lon + nlon - 1, nlon)
    has_south, has_north = lat > 0, lat < nlat - 1

    barrier = pltpu.get_barrier_semaphore()
    for side in (east, west):
        pl.semaphore_signal(barrier, inc=1, device_id={"lon": side}, device_id_type=MESH)

    @pl.when(has_south)
    def _():
        pl.semaphore_signal(barrier, inc=1, device_id={"lat": lat - 1}, device_id_type=MESH)

    @pl.when(has_north)
    def _():
        pl.semaphore_signal(barrier, inc=1, device_id={"lat": lat + 1}, device_id_type=MESH)

    @pl.when(jnp.logical_not(has_south))
    def _():
        south_ref[...] = jnp.zeros_like(south_ref)
        pl.semaphore_wait(barrier, 3)

    @pl.when(jnp.logical_not(has_north))
    def _():
        north_ref[...] = jnp.zeros_like(north_ref)
        pl.semaphore_wait(barrier, 3)

    @pl.when(jnp.logical_and(has_south, has_north))
    def _():
        pl.semaphore_wait(barrier, 4)

    groups = ((0, edge), (rows - edge, edge), (edge, rows - 2 * edge))

    def lon_copies(source, turn, group):
        first, number = groups[group]
        held = pl.ds(first, number)
        pairs = (
            (source.at[held, :, pl.ds(lanes - unit, unit)], west_ref.at[turn, held], east),
            (source.at[held, :, pl.ds(0, unit)], east_ref.at[turn, held], west),
        )
        return [
            pltpu.make_async_remote_copy(
                src_ref=src,
                dst_ref=dst,
                send_sem=lon_send.at[turn, group, way],
                recv_sem=lon_recv.at[turn, group, way],
                device_id={"lon": to},
                device_id_type=MESH,
            )
            for way, (src, dst, to) in enumerate(pairs)
        ]

    def lat_copies(source, turn):
        up = pltpu.make_async_remote_copy(
            src_ref=source.at[pl.ds(rows - edge, edge)],
            dst_ref=south_ref.at[turn],
            send_sem=lat_send.at[turn, 0],
            recv_sem=lat_recv.at[turn, 0],
            device_id={"lat": lat + 1},
            device_id_type=MESH,
        )
        down = pltpu.make_async_remote_copy(
            src_ref=source.at[pl.ds(0, edge)],
            dst_ref=north_ref.at[turn],
            send_sem=lat_send.at[turn, 1],
            recv_sem=lat_recv.at[turn, 1],
            device_id={"lat": lat - 1},
            device_id_type=MESH,
        )
        return up, down

    def lat_start(source, turn):
        up, down = lat_copies(source, turn)

        @pl.when(has_north)
        def _():
            up.start()

        @pl.when(has_south)
        def _():
            down.start()

    def lat_wait(source, turn):
        up, down = lat_copies(source, turn)

        @pl.when(has_north)
        def _():
            up.wait_send()
            down.wait_recv()

        @pl.when(has_south)
        def _():
            down.wait_send()
            up.wait_recv()

    def edge_row(i):
        return i + (i // edge) * (rows - 2 * edge)

    low = lax.broadcasted_iota(jnp.int32, (species, unit), 1) < unit // 2

    def lon_sweep(source, target, turn, number, row_of):
        def one(i, carry):
            row = row_of(i)

            def tile(j):
                if j < 0:
                    return west_ref[turn, row]
                if j == tiles:
                    return east_ref[turn, row]
                return source[row, :, j * unit : (j + 1) * unit]

            def swap(v):
                return pltpu.roll(v, unit // 2, 1)

            before, here = tile(-1), tile(0)
            swapped = swap(here)
            behind = jnp.where(low, swap(before), swapped)
            flux, turned, cell = None, None, None
            for j in range(tiles + 1):
                if j < tiles:
                    after = tile(j + 1)
                    after_swapped = swap(after)
                    ahead = jnp.where(low, swapped, after_swapped)
                else:
                    after, after_swapped, ahead = here, swapped, swapped
                at = slice(j * unit, (j + 1) * unit)
                c = lonc_ref[row, :, at]
                k = lonk_ref[row, :, at]
                now = face_flux(c, k, before, behind, here, ahead)
                now_turned = swap(now)
                if j > 0:
                    upper = jnp.where(low, turned, now_turned)
                    target[row, :, (j - 1) * unit : j * unit] = cell - (upper - flux)
                flux, turned, cell = now, now_turned, here
                before, here, behind, swapped = here, after, ahead, after_swapped
            return carry

        lax.fori_loop(0, number, one, 0)

    def lat_sweep(source, target, turn, spans):
        def one(j, carry):
            at = pl.ds(pl.multiple_of(j * unit, unit), unit)

            def cell(row):
                if row < 0:
                    return south_ref[turn, row + edge, :, at]
                if row >= rows:
                    return north_ref[turn, row - rows, :, at]
                return source[row, :, at]

            for first, last in spans:
                aa, a, b = cell(first - 2), cell(first - 1), cell(first)
                flux = None
                for row in range(first, last + 1):
                    bb = cell(row + 1)
                    c = latc_ref[row, :, at]
                    k = latk_ref[row, :, at]
                    now = face_flux(c, k, aa, a, b, bb)
                    if flux is not None:
                        target[row - 1, :, at] = a - (now - flux)
                    flux = now
                    aa, a, b = a, b, bb
            return carry

        lax.fori_loop(0, tiles, one, 0)

    wide = min(WIDE, lanes)
    pieces = lanes // wide

    def chemistry(number, row_of):
        def one(i, carry):
            row = row_of(i // pieces)
            start = pl.multiple_of((i % pieces) * wide, wide)
            at = pl.ds(start, wide)
            q = state_ref[row, :, at]
            sun = sun_ref[row, :, at]
            loss = loss_ref[...]
            for _ in range(CHEM):
                high = q.astype(jnp.bfloat16)
                rest = (q - high.astype(jnp.float32)).astype(jnp.bfloat16)
                both = jnp.dot(
                    w_ref[...],
                    jnp.concatenate([high, rest, high], 0),
                    preferred_element_type=jnp.float32,
                )
                q = (q + both[:species] + sun * both[species:]) / (1.0 + loss * q * q)
            spots = range(wide // unit)
            q = jnp.concatenate([q[:, t * unit : (t + 1) * unit] for t in spots], 0)
            high = q.astype(jnp.bfloat16)
            rest = (q - high.astype(jnp.float32)).astype(jnp.bfloat16)
            terms = jnp.concatenate([high, rest, high], 1)
            mixed = [None for t in spots]
            for n in range(0, KMAX, 2):
                both = jnp.dot(
                    terms,
                    power_ref[:, n * unit : (n + 2) * unit],
                    preferred_element_type=jnp.float32,
                )
                for t in spots:
                    held = slice(t * species, (t + 1) * species)
                    count = cnt_ref[row, :, pl.ds(start + t * unit, unit)]
                    v = both[held, :unit]
                    if n > 0:
                        v = jnp.where(count > n, v, mixed[t])
                    mixed[t] = jnp.where(count > n + 1, both[held, unit:], v)
            for t in spots:
                state_ref[row, :, pl.ds(start + t * unit, unit)] = mixed[t]
            return carry

        lax.fori_loop(0, number * pieces, one, 0)

    inner = rows - 2 * edge
    edge_spans = ((0, edge), (rows - edge, rows))
    inner_spans = ((edge, rows - edge),)

    def inner_row(i):
        return i + edge

    first = [lon_copies(x_ref, 0, group) for group in range(3)]
    for pair in first:
        for copy in pair:
            copy.start()
    build_powers(unit, mix_ref, power_ref)
    for pair in first[:2]:
        for copy in pair:
            copy.wait()
    lon_sweep(x_ref, mid_ref, 0, 2 * edge, edge_row)
    lat_start(mid_ref, 0)
    for copy in first[2]:
        copy.wait()
    lon_sweep(x_ref, mid_ref, 0, inner, inner_row)
    lat_sweep(mid_ref, state_ref, 0, inner_spans)
    chemistry(inner, inner_row)
    second = [lon_copies(state_ref, 1, group) for group in range(3)]
    for copy in second[2]:
        copy.start()
    lat_wait(mid_ref, 0)
    lat_sweep(mid_ref, state_ref, 0, edge_spans)
    chemistry(2 * edge, edge_row)
    for pair in second[:2]:
        for copy in pair:
            copy.start()
    for pair in second[:2]:
        for copy in pair:
            copy.wait()
    lon_sweep(state_ref, again_ref, 1, 2 * edge, edge_row)
    lat_start(again_ref, 1)
    for copy in second[2]:
        copy.wait()
    lon_sweep(state_ref, again_ref, 1, inner, inner_row)
    lat_sweep(again_ref, out_ref, 1, inner_spans)
    lat_wait(again_ref, 1)
    lat_sweep(again_ref, out_ref, 1, edge_spans)


def shifted(value, axis, steps):
    count = lax.axis_size(axis)
    return lax.ppermute(value, axis, [(i, (i + steps) % count) for i in range(count)])


def from_ahead(value, axis):
    count = lax.axis_size(axis)
    return lax.ppermute(value, axis, [(i + 1, i) for i in range(count - 1)])


def slopes(c, m):
    return jnp.where(c >= 0.0, 0.5 * (1.0 - c), -0.5 * (1.0 + c)) * m


def shards(
    tracers,
    courant,
    switches,
    day_flags,
    diffusion_counts,
    night_rates,
    photo_rates,
    level_light,
    self_loss,
    vertical_mixing,
):
    species, rows, lanes = tracers.shape
    levels = level_light.shape[0]
    columns = lanes // levels
    unit = 2 * levels
    f32 = jnp.float32
    nlat = lax.axis_size("lat")
    faces = jnp.concatenate([courant, switches.astype(f32)], 0)
    east_faces = shifted(faces[0::2, :, :1], "lon", -1)
    north_faces = from_ahead(faces[1::2, :1], "lat")
    lon_faces = jnp.concatenate([faces[0::2], east_faces, east_faces], 2)
    lat_faces = jnp.concatenate([faces[1::2], north_faces], 1)
    global_face = lax.axis_index("lat") * rows + jnp.arange(rows + 1, dtype=jnp.int32)
    valid = ((global_face >= 1) & (global_face < rows * nlat)).astype(f32)[:, None]
    lat_c = lat_faces[0] * valid
    spread = functools.partial(jnp.repeat, repeats=levels, axis=-1)
    lon_c = spread(lon_faces[0])
    lon_k = spread(slopes(lon_faces[0], lon_faces[1]))
    lat_k = spread(slopes(lat_c, lat_faces[1]))
    lat_c = spread(lat_c)
    sun = spread(day_flags.astype(f32)) * jnp.tile(level_light, columns)
    counts = spread(diffusion_counts)
    mixing = jnp.concatenate([vertical_mixing, jnp.zeros((1,), f32)])
    mixing = jnp.tile(mixing, 2)[None]
    rates = jnp.concatenate([night_rates, photo_rates], 0)
    top = lax.reduce_precision(rates, 8, 7)
    rest = (rates - top).astype(jnp.bfloat16)
    top = top.astype(jnp.bfloat16)
    weights = jnp.concatenate([top, top, rest], 1)
    block = (rows, species, lanes)
    out = pl.pallas_call(
        functools.partial(kernel, unit),
        out_shape=jax.ShapeDtypeStruct(block, f32),
        in_specs=[pl.BlockSpec(memory_space=pltpu.VMEM)] * 10,
        out_specs=pl.BlockSpec(memory_space=pltpu.VMEM),
        scratch_shapes=[
            pltpu.VMEM(block, f32),
            pltpu.VMEM(block, f32),
            pltpu.VMEM(block, f32),
            pltpu.VMEM((2, rows, species, unit), f32),
            pltpu.VMEM((2, rows, species, unit), f32),
            pltpu.VMEM((2, 2, species, lanes), f32),
            pltpu.VMEM((2, 2, species, lanes), f32),
            pltpu.VMEM((3 * unit, KMAX * unit), jnp.bfloat16),
            pltpu.SemaphoreType.DMA((2, 3, 2)),
            pltpu.SemaphoreType.DMA((2, 3, 2)),
            pltpu.SemaphoreType.DMA((2, 2)),
            pltpu.SemaphoreType.DMA((2, 2)),
        ],
        compiler_params=pltpu.CompilerParams(
            collective_id=0, has_side_effects=True, vmem_limit_bytes=48 * 1024 * 1024
        ),
    )(
        jnp.transpose(tracers, (1, 0, 2)),
        lon_c[:, None],
        lon_k[:, None],
        lat_c[:, None],
        lat_k[:, None],
        sun[:, None],
        counts[:, None],
        mixing,
        weights,
        self_loss[:, None],
    )
    return jnp.transpose(out, (1, 0, 2))


def solution(mesh):
    grid = P(None, "lat", "lon")
    plane = P("lat", "lon")
    in_specs = (grid, grid, grid, plane, plane, P(), P(), P(), P(), P())
    return jax.shard_map(shards, mesh=mesh, in_specs=in_specs, out_specs=grid, check_vma=False)
```

```python
import functools

import jax
import jax.numpy as jnp
from jax import lax
from jax.experimental import pallas as pl
from jax.experimental.pallas import tpu as pltpu
from jax.sharding import PartitionSpec as P

CHEM = 6
KMAX = 8
WIDE = 2048
MESH = pl.DeviceIdType.MESH


def minmod(x, y):
    return jnp.maximum(jnp.minimum(x, y), 0.0) + jnp.minimum(jnp.maximum(x, y), 0.0)


def face_flux(c, coef, aa, a, b, bb):
    pos = c >= 0.0
    x = jnp.where(pos, a - aa, bb - b)
    return c * (jnp.where(pos, a, b) + coef * minmod(x, b - a))


def build_powers(unit, mix_ref, power_ref):
    source = lax.broadcasted_iota(jnp.int32, (unit, unit), 0)
    target = lax.broadcasted_iota(jnp.int32, (unit, unit), 1)
    up = jnp.broadcast_to(mix_ref[...], (unit, unit))
    down = pltpu.roll(up, 1, 1)
    one = jnp.where(source == target, 1.0 - up - down, 0.0)
    one = jnp.where(source == target + 1, up, one)
    one = jnp.where(source == target - 1, down, one)
    powers = {1: one}
    for n in range(2, KMAX + 1):
        half = n // 2
        powers[n] = jnp.dot(
            powers[half],
            powers[n - half],
            precision=lax.Precision.HIGHEST,
            preferred_element_type=jnp.float32,
        )
    for n, power in powers.items():
        at = slice((n - 1) * unit, n * unit)
        top = power.astype(jnp.bfloat16)
        power_ref[:unit, at] = top
        power_ref[unit : 2 * unit, at] = top
        power_ref[2 * unit :, at] = (power - top.astype(jnp.float32)).astype(jnp.bfloat16)


def kernel(
    unit,
    x_ref,
    courant_ref,
    switch_ref,
    day_ref,
    raw_cnt_ref,
    night_ref,
    photo_ref,
    light_ref,
    raw_loss_ref,
    vertical_ref,
    out_ref,
    lonc_ref,
    lonk_ref,
    latc_ref,
    latk_ref,
    sun_ref,
    cnt_ref,
    mix_ref,
    w_ref,
    loss_ref,
    face_c_ref,
    face_s_ref,
    mid_ref,
    state_ref,
    again_ref,
    west_ref,
    east_ref,
    south_ref,
    north_ref,
    power_ref,
    lon_send,
    lon_recv,
    lat_send,
    lat_recv,
    face_send,
    face_recv,
):
    rows, species, lanes = x_ref.shape
    tiles = lanes // unit
    edge = 2
    nlon, nlat = lax.axis_size("lon"), lax.axis_size("lat")
    lon, lat = lax.axis_index("lon"), lax.axis_index("lat")
    east, west = lax.rem(lon + 1, nlon), lax.rem(lon + nlon - 1, nlon)
    has_south, has_north = lat > 0, lat < nlat - 1

    barrier = pltpu.get_barrier_semaphore()
    for side in (east, west):
        pl.semaphore_signal(barrier, inc=1, device_id={"lon": side}, device_id_type=MESH)

    @pl.when(has_south)
    def _():
        pl.semaphore_signal(barrier, inc=1, device_id={"lat": lat - 1}, device_id_type=MESH)

    @pl.when(has_north)
    def _():
        pl.semaphore_signal(barrier, inc=1, device_id={"lat": lat + 1}, device_id_type=MESH)

    @pl.when(jnp.logical_not(has_south))
    def _():
        south_ref[...] = jnp.zeros_like(south_ref)
        pl.semaphore_wait(barrier, 3)

    @pl.when(jnp.logical_not(has_north))
    def _():
        north_ref[...] = jnp.zeros_like(north_ref)
        face_c_ref[1] = jnp.zeros(face_c_ref.shape[1:], face_c_ref.dtype)
        face_s_ref[1] = jnp.zeros(face_s_ref.shape[1:], face_s_ref.dtype)
        pl.semaphore_wait(barrier, 3)

    @pl.when(jnp.logical_and(has_south, has_north))
    def _():
        pl.semaphore_wait(barrier, 4)

    groups = ((0, edge), (rows - edge, edge), (edge, rows - 2 * edge))

    def lon_copies(source, turn, group):
        first, number = groups[group]
        held = pl.ds(first, number)
        pairs = (
            (source.at[held, :, pl.ds(lanes - unit, unit)], west_ref.at[turn, held], east),
            (source.at[held, :, pl.ds(0, unit)], east_ref.at[turn, held], west),
        )
        return [
            pltpu.make_async_remote_copy(
                src_ref=src,
                dst_ref=dst,
                send_sem=lon_send.at[turn, group, way],
                recv_sem=lon_recv.at[turn, group, way],
                device_id={"lon": to},
                device_id_type=MESH,
            )
            for way, (src, dst, to) in enumerate(pairs)
        ]

    def face_copies(side, to):
        pairs = ((courant_ref, face_c_ref), (switch_ref, face_s_ref))
        return [
            pltpu.make_async_remote_copy(
                src_ref=src,
                dst_ref=dst.at[side],
                send_sem=face_send.at[side, n],
                recv_sem=face_recv.at[side, n],
                device_id=to,
                device_id_type=MESH,
            )
            for n, (src, dst) in enumerate(pairs)
        ]

    lon_faces = face_copies(0, {"lon": west})
    lat_faces = face_copies(1, {"lat": lat - 1})

    def spread(plane, target, scale=None):
        left = lax.broadcasted_iota(jnp.int32, (plane.shape[0], unit), 1) < unit // 2
        for j in range(tiles):
            a = jnp.broadcast_to(plane[:, 2 * j : 2 * j + 1], left.shape)
            b = jnp.broadcast_to(plane[:, 2 * j + 1 : 2 * j + 2], left.shape)
            v = jnp.where(left, a, b)
            if scale is not None:
                v = v * scale
            for r in range(plane.shape[0]):
                target(r, slice(j * unit, (j + 1) * unit), v[r : r + 1])

    def into(ref, offset=0):
        def put(r, at, v):
            ref[r + offset, :, at] = v

        return put

    def prepare():
        c = courant_ref[...]
        m = switch_ref[...].astype(jnp.float32)
        spread(c[0], into(lonc_ref))
        spread(slopes(c[0], m[0]), into(lonk_ref))
        row = lax.broadcasted_iota(jnp.int32, c[1].shape, 0)
        lat_c = jnp.where(jnp.logical_and(row == 0, lat == 0), 0.0, c[1])
        spread(lat_c, into(latc_ref))
        spread(slopes(lat_c, m[1]), into(latk_ref))
        mix = vertical_ref[...]
        gap = jnp.zeros((1, 1), jnp.float32)
        mix_ref[...] = jnp.concatenate([mix, gap, mix, gap], 1)
        light = jnp.concatenate([light_ref[...], light_ref[...]], 1)
        spread(day_ref[...].astype(jnp.float32), into(sun_ref), light)
        spread(raw_cnt_ref[...], into(cnt_ref))

    def prepare_outer():
        c = face_c_ref[0, 0][:, :1]
        k = slopes(c, face_s_ref[0, 0][:, :1].astype(jnp.float32))
        c = jnp.broadcast_to(c, (rows, unit))
        k = jnp.broadcast_to(k, (rows, unit))
        for r in range(rows):
            lonc_ref[r, :, lanes:] = c[r : r + 1]
            lonk_ref[r, :, lanes:] = k[r : r + 1]

    def prepare_north():
        c = face_c_ref[1, 1][:1]
        spread(c, into(latc_ref, rows))
        spread(slopes(c, face_s_ref[1, 1][:1].astype(jnp.float32)), into(latk_ref, rows))

    def prepare_rates():
        rates = jnp.concatenate([night_ref[...], photo_ref[...]], 0)
        top = rates.astype(jnp.bfloat16).astype(jnp.float32)
        w_ref[...] = jnp.concatenate([top, top, rates - top], 1).astype(jnp.bfloat16)
        shape = (species, species)
        same = lax.broadcasted_iota(jnp.int32, shape, 0) == lax.broadcasted_iota(jnp.int32, shape, 1)
        spread_loss = jnp.broadcast_to(raw_loss_ref[...], shape)
        loss_ref[...] = jnp.sum(jnp.where(same, spread_loss, 0.0), axis=1, keepdims=True)

    def lat_copies(source, turn):
        up = pltpu.make_async_remote_copy(
            src_ref=source.at[pl.ds(rows - edge, edge)],
            dst_ref=south_ref.at[turn],
            send_sem=lat_send.at[turn, 0],
            recv_sem=lat_recv.at[turn, 0],
            device_id={"lat": lat + 1},
            device_id_type=MESH,
        )
        down = pltpu.make_async_remote_copy(
            src_ref=source.at[pl.ds(0, edge)],
            dst_ref=north_ref.at[turn],
            send_sem=lat_send.at[turn, 1],
            recv_sem=lat_recv.at[turn, 1],
            device_id={"lat": lat - 1},
            device_id_type=MESH,
        )
        return up, down

    def lat_start(source, turn):
        up, down = lat_copies(source, turn)

        @pl.when(has_north)
        def _():
            up.start()

        @pl.when(has_south)
        def _():
            down.start()

    def lat_wait(source, turn):
        up, down = lat_copies(source, turn)

        @pl.when(has_north)
        def _():
            up.wait_send()
            down.wait_recv()

        @pl.when(has_south)
        def _():
            down.wait_send()
            up.wait_recv()

    def edge_row(i):
        return i + (i // edge) * (rows - 2 * edge)

    low = lax.broadcasted_iota(jnp.int32, (species, unit), 1) < unit // 2

    def lon_sweep(source, target, turn, number, row_of):
        def one(i, carry):
            row = row_of(i)

            def tile(j):
                if j < 0:
                    return west_ref[turn, row]
                if j == tiles:
                    return east_ref[turn, row]
                return source[row, :, j * unit : (j + 1) * unit]

            def swap(v):
                return pltpu.roll(v, unit // 2, 1)

            before, here = tile(-1), tile(0)
            swapped = swap(here)
            behind = jnp.where(low, swap(before), swapped)
            flux, turned, cell = None, None, None
            for j in range(tiles + 1):
                if j < tiles:
                    after = tile(j + 1)
                    after_swapped = swap(after)
                    ahead = jnp.where(low, swapped, after_swapped)
                else:
                    after, after_swapped, ahead = here, swapped, swapped
                at = slice(j * unit, (j + 1) * unit)
                c = lonc_ref[row, :, at]
                k = lonk_ref[row, :, at]
                now = face_flux(c, k, before, behind, here, ahead)
                now_turned = swap(now)
                if j > 0:
                    upper = jnp.where(low, turned, now_turned)
                    target[row, :, (j - 1) * unit : j * unit] = cell - (upper - flux)
                flux, turned, cell = now, now_turned, here
                before, here, behind, swapped = here, after, ahead, after_swapped
            return carry

        lax.fori_loop(0, number, one, 0)

    def lat_sweep(source, target, turn, spans):
        def one(j, carry):
            at = pl.ds(pl.multiple_of(j * unit, unit), unit)

            def cell(row):
                if row < 0:
                    return south_ref[turn, row + edge, :, at]
                if row >= rows:
                    return north_ref[turn, row - rows, :, at]
                return source[row, :, at]

            for first, last in spans:
                aa, a, b = cell(first - 2), cell(first - 1), cell(first)
                flux = None
                for row in range(first, last + 1):
                    bb = cell(row + 1)
                    c = latc_ref[row, :, at]
                    k = latk_ref[row, :, at]
                    now = face_flux(c, k, aa, a, b, bb)
                    if flux is not None:
                        target[row - 1, :, at] = a - (now - flux)
                    flux = now
                    aa, a, b = a, b, bb
            return carry

        lax.fori_loop(0, tiles, one, 0)

    wide = min(WIDE, lanes)
    pieces = lanes // wide

    def chemistry(number, row_of):
        def one(i, carry):
            row = row_of(i // pieces)
            start = pl.multiple_of((i % pieces) * wide, wide)
            at = pl.ds(start, wide)
            q = state_ref[row, :, at]
            sun = sun_ref[row, :, at]
            loss = loss_ref[...]
            for _ in range(CHEM):
                high = q.astype(jnp.bfloat16)
                rest = (q - high.astype(jnp.float32)).astype(jnp.bfloat16)
                both = jnp.dot(
                    w_ref[...],
                    jnp.concatenate([high, rest, high], 0),
                    preferred_element_type=jnp.float32,
                )
                q = (q + both[:species] + sun * both[species:]) / (1.0 + loss * q * q)
            spots = range(wide // unit)
            q = jnp.concatenate([q[:, t * unit : (t + 1) * unit] for t in spots], 0)
            high = q.astype(jnp.bfloat16)
            rest = (q - high.astype(jnp.float32)).astype(jnp.bfloat16)
            terms = jnp.concatenate([high, rest, high], 1)
            mixed = [None for t in spots]
            for n in range(0, KMAX, 2):
                both = jnp.dot(
                    terms,
                    power_ref[:, n * unit : (n + 2) * unit],
                    preferred_element_type=jnp.float32,
                )
                for t in spots:
                    held = slice(t * species, (t + 1) * species)
                    count = cnt_ref[row, :, pl.ds(start + t * unit, unit)]
                    v = both[held, :unit]
                    if n > 0:
                        v = jnp.where(count > n, v, mixed[t])
                    mixed[t] = jnp.where(count > n + 1, both[held, unit:], v)
            for t in spots:
                state_ref[row, :, pl.ds(start + t * unit, unit)] = mixed[t]
            return carry

        lax.fori_loop(0, number * pieces, one, 0)

    inner = rows - 2 * edge
    edge_spans = ((0, edge), (rows - edge, rows))
    inner_spans = ((edge, rows - edge),)

    def inner_row(i):
        return i + edge

    for copy in lon_faces:
        copy.start()

    @pl.when(has_south)
    def _():
        for copy in lat_faces:
            copy.start()

    first = [lon_copies(x_ref, 0, group) for group in range(3)]
    for pair in first:
        for copy in pair:
            copy.start()
    prepare()
    for copy in lon_faces:
        copy.wait()
    prepare_outer()
    for pair in first[:2]:
        for copy in pair:
            copy.wait()
    lon_sweep(x_ref, mid_ref, 0, 2 * edge, edge_row)
    lat_start(mid_ref, 0)
    prepare_rates()
    build_powers(unit, mix_ref, power_ref)

    @pl.when(has_south)
    def _():
        for copy in lat_faces:
            copy.wait_send()

    @pl.when(has_north)
    def _():
        for copy in lat_faces:
            copy.wait_recv()

    prepare_north()
    for copy in first[2]:
        copy.wait()
    lon_sweep(x_ref, mid_ref, 0, inner, inner_row)
    lat_sweep(mid_ref, state_ref, 0, inner_spans)
    chemistry(inner, inner_row)
    second = [lon_copies(state_ref, 1, group) for group in range(3)]
    for copy in second[2]:
        copy.start()
    lat_wait(mid_ref, 0)
    lat_sweep(mid_ref, state_ref, 0, edge_spans)
    chemistry(2 * edge, edge_row)
    for pair in second[:2]:
        for copy in pair:
            copy.start()
    for pair in second[:2]:
        for copy in pair:
            copy.wait()
    lon_sweep(state_ref, again_ref, 1, 2 * edge, edge_row)
    lat_start(again_ref, 1)
    for copy in second[2]:
        copy.wait()
    lon_sweep(state_ref, again_ref, 1, inner, inner_row)
    lat_sweep(again_ref, out_ref, 1, inner_spans)
    lat_wait(again_ref, 1)
    lat_sweep(again_ref, out_ref, 1, edge_spans)


def slopes(c, m):
    return jnp.where(c >= 0.0, 0.5 * (1.0 - c), -0.5 * (1.0 + c)) * m


def shards(
    tracers,
    courant,
    switches,
    day_flags,
    diffusion_counts,
    night_rates,
    photo_rates,
    level_light,
    self_loss,
    vertical_mixing,
):
    species, rows, lanes = tracers.shape
    levels = level_light.shape[0]
    unit = 2 * levels
    f32, i32, bf16 = jnp.float32, jnp.int32, jnp.bfloat16
    block = (rows, species, lanes)
    out = pl.pallas_call(
        functools.partial(kernel, unit),
        out_shape=jax.ShapeDtypeStruct(block, f32),
        in_specs=[pl.BlockSpec(memory_space=pltpu.VMEM)] * 10,
        out_specs=pl.BlockSpec(memory_space=pltpu.VMEM),
        scratch_shapes=[
            pltpu.VMEM((rows, 1, lanes + unit), f32),
            pltpu.VMEM((rows, 1, lanes + unit), f32),
            pltpu.VMEM((rows + 1, 1, lanes), f32),
            pltpu.VMEM((rows + 1, 1, lanes), f32),
            pltpu.VMEM((rows, 1, lanes), f32),
            pltpu.VMEM((rows, 1, lanes), i32),
            pltpu.VMEM((1, unit), f32),
            pltpu.VMEM((2 * species, 3 * species), bf16),
            pltpu.VMEM((species, 1), f32),
            pltpu.VMEM((2,) + courant.shape, f32),
            pltpu.VMEM((2,) + switches.shape, i32),
            pltpu.VMEM(block, f32),
            pltpu.VMEM(block, f32),
            pltpu.VMEM(block, f32),
            pltpu.VMEM((2, rows, species, unit), f32),
            pltpu.VMEM((2, rows, species, unit), f32),
            pltpu.VMEM((2, 2, species, lanes), f32),
            pltpu.VMEM((2, 2, species, lanes), f32),
            pltpu.VMEM((3 * unit, KMAX * unit), bf16),
            pltpu.SemaphoreType.DMA((2, 3, 2)),
            pltpu.SemaphoreType.DMA((2, 3, 2)),
            pltpu.SemaphoreType.DMA((2, 2)),
            pltpu.SemaphoreType.DMA((2, 2)),
            pltpu.SemaphoreType.DMA((2, 2)),
            pltpu.SemaphoreType.DMA((2, 2)),
        ],
        compiler_params=pltpu.CompilerParams(
            collective_id=0, has_side_effects=True, vmem_limit_bytes=48 * 1024 * 1024
        ),
    )(
        jnp.transpose(tracers, (1, 0, 2)),
        courant,
        switches,
        day_flags,
        diffusion_counts,
        night_rates,
        photo_rates,
        level_light[None],
        self_loss[None],
        vertical_mixing[None],
    )
    return jnp.transpose(out, (1, 0, 2))


def solution(mesh):
    grid = P(None, "lat", "lon")
    plane = P("lat", "lon")
    in_specs = (grid, grid, grid, plane, plane, P(), P(), P(), P(), P())
    return jax.shard_map(shards, mesh=mesh, in_specs=in_specs, out_specs=grid, check_vma=False)
```

```python
import functools

import jax
import jax.numpy as jnp
from jax import lax
from jax.experimental import pallas as pl
from jax.experimental.pallas import tpu as pltpu
from jax.sharding import PartitionSpec as P

CHEM = 6
KMAX = 8
WIDE = 2048
MESH = pl.DeviceIdType.MESH


def minmod(x, y):
    return jnp.maximum(jnp.minimum(x, y), 0.0) + jnp.minimum(jnp.maximum(x, y), 0.0)


def face_flux(c, coef, aa, a, b, bb):
    pos = c >= 0.0
    x = jnp.where(pos, a - aa, bb - b)
    return c * (jnp.where(pos, a, b) + coef * minmod(x, b - a))


def build_powers(unit, mix_ref, power_ref):
    source = lax.broadcasted_iota(jnp.int32, (unit, unit), 0)
    target = lax.broadcasted_iota(jnp.int32, (unit, unit), 1)
    up = jnp.broadcast_to(mix_ref[...], (unit, unit))
    down = pltpu.roll(up, 1, 1)
    one = jnp.where(source == target, 1.0 - up - down, 0.0)
    one = jnp.where(source == target + 1, up, one)
    one = jnp.where(source == target - 1, down, one)
    powers = {1: one}
    for n in range(2, KMAX + 1):
        half = n // 2
        powers[n] = jnp.dot(
            powers[half],
            powers[n - half],
            precision=lax.Precision.HIGHEST,
            preferred_element_type=jnp.float32,
        )
    for n, power in powers.items():
        at = slice((n - 1) * unit, n * unit)
        top = power.astype(jnp.bfloat16)
        power_ref[:unit, at] = top
        power_ref[unit : 2 * unit, at] = top
        power_ref[2 * unit :, at] = (power - top.astype(jnp.float32)).astype(jnp.bfloat16)


def kernel(
    unit,
    x_ref,
    courant_ref,
    switch_ref,
    day_ref,
    raw_cnt_ref,
    night_ref,
    photo_ref,
    light_ref,
    raw_loss_ref,
    vertical_ref,
    out_ref,
    lonc_ref,
    lonk_ref,
    latc_ref,
    latk_ref,
    sun_ref,
    cnt_ref,
    mix_ref,
    w_ref,
    loss_ref,
    face_c_ref,
    face_s_ref,
    mid_ref,
    state_ref,
    again_ref,
    west_ref,
    east_ref,
    south_ref,
    north_ref,
    power_ref,
    lon_send,
    lon_recv,
    lat_send,
    lat_recv,
    face_send,
    face_recv,
):
    rows, species, lanes = x_ref.shape
    tiles = lanes // unit
    edge = 2
    nlon, nlat = lax.axis_size("lon"), lax.axis_size("lat")
    lon, lat = lax.axis_index("lon"), lax.axis_index("lat")
    east, west = lax.rem(lon + 1, nlon), lax.rem(lon + nlon - 1, nlon)
    has_south, has_north = lat > 0, lat < nlat - 1
    lower_half = lat < nlat // 2

    barrier = pltpu.get_barrier_semaphore()
    for side in (east, west):
        pl.semaphore_signal(barrier, inc=1, device_id={"lon": side}, device_id_type=MESH)

    @pl.when(has_south)
    def _():
        pl.semaphore_signal(barrier, inc=1, device_id={"lat": lat - 1}, device_id_type=MESH)

    @pl.when(has_north)
    def _():
        pl.semaphore_signal(barrier, inc=1, device_id={"lat": lat + 1}, device_id_type=MESH)

    @pl.when(jnp.logical_not(has_south))
    def _():
        south_ref[...] = jnp.zeros_like(south_ref)
        pl.semaphore_wait(barrier, 3)

    @pl.when(jnp.logical_not(has_north))
    def _():
        north_ref[...] = jnp.zeros_like(north_ref)
        face_c_ref[1] = jnp.zeros(face_c_ref.shape[1:], face_c_ref.dtype)
        face_s_ref[1] = jnp.zeros(face_s_ref.shape[1:], face_s_ref.dtype)
        pl.semaphore_wait(barrier, 3)

    @pl.when(jnp.logical_and(has_south, has_north))
    def _():
        pl.semaphore_wait(barrier, 4)

    groups = ((0, edge), (rows - edge, edge), (edge, rows - 2 * edge))

    def lon_copies(source, turn, group):
        first, number = groups[group]
        held = pl.ds(first, number)
        pairs = (
            (source.at[held, :, pl.ds(lanes - unit, unit)], west_ref.at[turn, held], east),
            (source.at[held, :, pl.ds(0, unit)], east_ref.at[turn, held], west),
        )
        return [
            pltpu.make_async_remote_copy(
                src_ref=src,
                dst_ref=dst,
                send_sem=lon_send.at[turn, group, way],
                recv_sem=lon_recv.at[turn, group, way],
                device_id={"lon": to},
                device_id_type=MESH,
            )
            for way, (src, dst, to) in enumerate(pairs)
        ]

    def face_copies(side, to):
        pairs = ((courant_ref, face_c_ref), (switch_ref, face_s_ref))
        return [
            pltpu.make_async_remote_copy(
                src_ref=src,
                dst_ref=dst.at[side],
                send_sem=face_send.at[side, n],
                recv_sem=face_recv.at[side, n],
                device_id=to,
                device_id_type=MESH,
            )
            for n, (src, dst) in enumerate(pairs)
        ]

    lon_faces = face_copies(0, {"lon": west})
    lat_faces = face_copies(1, {"lat": lat - 1})

    def spread(plane, target, scale=None):
        left = lax.broadcasted_iota(jnp.int32, (plane.shape[0], unit), 1) < unit // 2
        for j in range(tiles):
            a = jnp.broadcast_to(plane[:, 2 * j : 2 * j + 1], left.shape)
            b = jnp.broadcast_to(plane[:, 2 * j + 1 : 2 * j + 2], left.shape)
            v = jnp.where(left, a, b)
            if scale is not None:
                v = v * scale
            for r in range(plane.shape[0]):
                target(r, slice(j * unit, (j + 1) * unit), v[r : r + 1])

    def into(ref, offset=0):
        def put(r, at, v):
            ref[r + offset, :, at] = v

        return put

    def prepare():
        c = courant_ref[...]
        m = switch_ref[...].astype(jnp.float32)
        spread(c[0], into(lonc_ref))
        spread(slopes(c[0], m[0]), into(lonk_ref))
        row = lax.broadcasted_iota(jnp.int32, c[1].shape, 0)
        lat_c = jnp.where(jnp.logical_and(row == 0, lat == 0), 0.0, c[1])
        spread(lat_c, into(latc_ref))
        spread(slopes(lat_c, m[1]), into(latk_ref))
        mix = vertical_ref[...]
        gap = jnp.zeros((1, 1), jnp.float32)
        mix_ref[...] = jnp.concatenate([mix, gap, mix, gap], 1)
        light = jnp.concatenate([light_ref[...], light_ref[...]], 1)
        spread(day_ref[...].astype(jnp.float32), into(sun_ref), light)
        spread(raw_cnt_ref[...], into(cnt_ref))

    def prepare_outer():
        c = face_c_ref[0, 0][:, :1]
        k = slopes(c, face_s_ref[0, 0][:, :1].astype(jnp.float32))
        c = jnp.broadcast_to(c, (rows, unit))
        k = jnp.broadcast_to(k, (rows, unit))
        for r in range(rows):
            lonc_ref[r, :, lanes:] = c[r : r + 1]
            lonk_ref[r, :, lanes:] = k[r : r + 1]

    def prepare_north():
        c = face_c_ref[1, 1][:1]
        spread(c, into(latc_ref, rows))
        spread(slopes(c, face_s_ref[1, 1][:1].astype(jnp.float32)), into(latk_ref, rows))

    def prepare_rates():
        rates = jnp.concatenate([night_ref[...], photo_ref[...]], 0)
        top = rates.astype(jnp.bfloat16).astype(jnp.float32)
        w_ref[...] = jnp.concatenate([top, top, rates - top], 1).astype(jnp.bfloat16)
        shape = (species, species)
        same = lax.broadcasted_iota(jnp.int32, shape, 0) == lax.broadcasted_iota(jnp.int32, shape, 1)
        spread_loss = jnp.broadcast_to(raw_loss_ref[...], shape)
        loss_ref[...] = jnp.sum(jnp.where(same, spread_loss, 0.0), axis=1, keepdims=True)

    def lat_copies(source, turn):
        up = pltpu.make_async_remote_copy(
            src_ref=source.at[pl.ds(rows - edge, edge)],
            dst_ref=south_ref.at[turn],
            send_sem=lat_send.at[turn, 0],
            recv_sem=lat_recv.at[turn, 0],
            device_id={"lat": lat + 1},
            device_id_type=MESH,
        )
        down = pltpu.make_async_remote_copy(
            src_ref=source.at[pl.ds(0, edge)],
            dst_ref=north_ref.at[turn],
            send_sem=lat_send.at[turn, 1],
            recv_sem=lat_recv.at[turn, 1],
            device_id={"lat": lat - 1},
            device_id_type=MESH,
        )
        return up, down

    def lat_start(source, turn):
        up, down = lat_copies(source, turn)

        @pl.when(jnp.logical_and(has_north, lower_half))
        def _():
            up.start()

        @pl.when(has_south)
        def _():
            down.start()

        @pl.when(jnp.logical_and(has_north, jnp.logical_not(lower_half)))
        def _():
            up.start()

    def lat_arrive(source, turn, side):
        up, down = lat_copies(source, turn)

        @pl.when(has_north if side else has_south)
        def _():
            (down if side else up).wait_recv()

    def lat_sent(source, turn):
        up, down = lat_copies(source, turn)

        @pl.when(has_north)
        def _():
            up.wait_send()

        @pl.when(has_south)
        def _():
            down.wait_send()

    def edge_row(i):
        return i + (i // edge) * (rows - 2 * edge)

    low = lax.broadcasted_iota(jnp.int32, (species, unit), 1) < unit // 2

    def lon_sweep(source, target, turn, number, row_of):
        def one(i, carry):
            row = row_of(i)

            def tile(j):
                if j < 0:
                    return west_ref[turn, row]
                if j == tiles:
                    return east_ref[turn, row]
                return source[row, :, j * unit : (j + 1) * unit]

            def swap(v):
                return pltpu.roll(v, unit // 2, 1)

            before, here = tile(-1), tile(0)
            swapped = swap(here)
            behind = jnp.where(low, swap(before), swapped)
            flux, turned, cell = None, None, None
            for j in range(tiles + 1):
                if j < tiles:
                    after = tile(j + 1)
                    after_swapped = swap(after)
                    ahead = jnp.where(low, swapped, after_swapped)
                else:
                    after, after_swapped, ahead = here, swapped, swapped
                at = slice(j * unit, (j + 1) * unit)
                c = lonc_ref[row, :, at]
                k = lonk_ref[row, :, at]
                now = face_flux(c, k, before, behind, here, ahead)
                now_turned = swap(now)
                if j > 0:
                    upper = jnp.where(low, turned, now_turned)
                    target[row, :, (j - 1) * unit : j * unit] = cell - (upper - flux)
                flux, turned, cell = now, now_turned, here
                before, here, behind, swapped = here, after, ahead, after_swapped
            return carry

        lax.fori_loop(0, number, one, 0)

    def lat_sweep(source, target, turn, spans):
        def one(j, carry):
            at = pl.ds(pl.multiple_of(j * unit, unit), unit)

            def cell(row):
                if row < 0:
                    return south_ref[turn, row + edge, :, at]
                if row >= rows:
                    return north_ref[turn, row - rows, :, at]
                return source[row, :, at]

            for first, last in spans:
                aa, a, b = cell(first - 2), cell(first - 1), cell(first)
                flux = None
                for row in range(first, last + 1):
                    bb = cell(row + 1)
                    c = latc_ref[row, :, at]
                    k = latk_ref[row, :, at]
                    now = face_flux(c, k, aa, a, b, bb)
                    if flux is not None:
                        target[row - 1, :, at] = a - (now - flux)
                    flux = now
                    aa, a, b = a, b, bb
            return carry

        lax.fori_loop(0, tiles, one, 0)

    wide = min(WIDE, lanes)
    pieces = lanes // wide

    def chemistry(number, row_of):
        def one(i, carry):
            row = row_of(i // pieces)
            start = pl.multiple_of((i % pieces) * wide, wide)
            at = pl.ds(start, wide)
            q = state_ref[row, :, at]
            sun = sun_ref[row, :, at]
            loss = loss_ref[...]
            for _ in range(CHEM):
                high = q.astype(jnp.bfloat16)
                rest = (q - high.astype(jnp.float32)).astype(jnp.bfloat16)
                both = jnp.dot(
                    w_ref[...],
                    jnp.concatenate([high, rest, high], 0),
                    preferred_element_type=jnp.float32,
                )
                q = (q + both[:species] + sun * both[species:]) / (1.0 + loss * q * q)
            spots = range(wide // unit)
            q = jnp.concatenate([q[:, t * unit : (t + 1) * unit] for t in spots], 0)
            high = q.astype(jnp.bfloat16)
            rest = (q - high.astype(jnp.float32)).astype(jnp.bfloat16)
            terms = jnp.concatenate([high, rest, high], 1)
            mixed = [None for t in spots]
            for n in range(0, KMAX, 2):
                both = jnp.dot(
                    terms,
                    power_ref[:, n * unit : (n + 2) * unit],
                    preferred_element_type=jnp.float32,
                )
                for t in spots:
                    held = slice(t * species, (t + 1) * species)
                    count = cnt_ref[row, :, pl.ds(start + t * unit, unit)]
                    v = both[held, :unit]
                    if n > 0:
                        v = jnp.where(count > n, v, mixed[t])
                    mixed[t] = jnp.where(count > n + 1, both[held, unit:], v)
            for t in spots:
                state_ref[row, :, pl.ds(start + t * unit, unit)] = mixed[t]
            return carry

        lax.fori_loop(0, number * pieces, one, 0)

    inner = rows - 2 * edge
    edge_spans = ((0, edge), (rows - edge, rows))
    inner_spans = ((edge, rows - edge),)

    def inner_row(i):
        return i + edge

    for copy in lon_faces:
        copy.start()

    @pl.when(has_south)
    def _():
        for copy in lat_faces:
            copy.start()

    first = [lon_copies(x_ref, 0, group) for group in range(3)]
    for pair in first:
        for copy in pair:
            copy.start()
    prepare()
    for copy in lon_faces:
        copy.wait()
    prepare_outer()
    for pair in first[:2]:
        for copy in pair:
            copy.wait()
    lon_sweep(x_ref, mid_ref, 0, 2 * edge, edge_row)
    lat_start(mid_ref, 0)
    prepare_rates()
    build_powers(unit, mix_ref, power_ref)

    @pl.when(has_south)
    def _():
        for copy in lat_faces:
            copy.wait_send()

    @pl.when(has_north)
    def _():
        for copy in lat_faces:
            copy.wait_recv()

    prepare_north()
    for copy in first[2]:
        copy.wait()
    lon_sweep(x_ref, mid_ref, 0, inner, inner_row)
    lat_sweep(mid_ref, state_ref, 0, inner_spans)
    chemistry(inner, inner_row)
    second = [lon_copies(state_ref, 1, group) for group in range(3)]
    for copy in second[2]:
        copy.start()

    def finish_edge(side):
        lat_arrive(mid_ref, 0, side)
        lat_sweep(mid_ref, state_ref, 0, (edge_spans[side],))
        chemistry(edge, lambda i: i + side * (rows - edge))
        for copy in second[side]:
            copy.start()

    @pl.when(lower_half)
    def _():
        finish_edge(0)
        finish_edge(1)

    @pl.when(jnp.logical_not(lower_half))
    def _():
        finish_edge(1)
        finish_edge(0)

    for pair in second[:2]:
        for copy in pair:
            copy.wait()
    lon_sweep(state_ref, again_ref, 1, 2 * edge, edge_row)
    lat_start(again_ref, 1)
    for copy in second[2]:
        copy.wait()
    lon_sweep(state_ref, again_ref, 1, inner, inner_row)
    lat_sweep(again_ref, out_ref, 1, inner_spans)
    for side in range(2):
        lat_arrive(again_ref, 1, side)
        lat_sweep(again_ref, out_ref, 1, (edge_spans[side],))
    lat_sent(mid_ref, 0)
    lat_sent(again_ref, 1)


def slopes(c, m):
    return jnp.where(c >= 0.0, 0.5 * (1.0 - c), -0.5 * (1.0 + c)) * m


def shards(
    tracers,
    courant,
    switches,
    day_flags,
    diffusion_counts,
    night_rates,
    photo_rates,
    level_light,
    self_loss,
    vertical_mixing,
):
    species, rows, lanes = tracers.shape
    levels = level_light.shape[0]
    unit = 2 * levels
    f32, i32, bf16 = jnp.float32, jnp.int32, jnp.bfloat16
    block = (rows, species, lanes)
    out = pl.pallas_call(
        functools.partial(kernel, unit),
        out_shape=jax.ShapeDtypeStruct(block, f32),
        in_specs=[pl.BlockSpec(memory_space=pltpu.VMEM)] * 10,
        out_specs=pl.BlockSpec(memory_space=pltpu.VMEM),
        scratch_shapes=[
            pltpu.VMEM((rows, 1, lanes + unit), f32),
            pltpu.VMEM((rows, 1, lanes + unit), f32),
            pltpu.VMEM((rows + 1, 1, lanes), f32),
            pltpu.VMEM((rows + 1, 1, lanes), f32),
            pltpu.VMEM((rows, 1, lanes), f32),
            pltpu.VMEM((rows, 1, lanes), i32),
            pltpu.VMEM((1, unit), f32),
            pltpu.VMEM((2 * species, 3 * species), bf16),
            pltpu.VMEM((species, 1), f32),
            pltpu.VMEM((2,) + courant.shape, f32),
            pltpu.VMEM((2,) + switches.shape, i32),
            pltpu.VMEM(block, f32),
            pltpu.VMEM(block, f32),
            pltpu.VMEM(block, f32),
            pltpu.VMEM((2, rows, species, unit), f32),
            pltpu.VMEM((2, rows, species, unit), f32),
            pltpu.VMEM((2, 2, species, lanes), f32),
            pltpu.VMEM((2, 2, species, lanes), f32),
            pltpu.VMEM((3 * unit, KMAX * unit), bf16),
            pltpu.SemaphoreType.DMA((2, 3, 2)),
            pltpu.SemaphoreType.DMA((2, 3, 2)),
            pltpu.SemaphoreType.DMA((2, 2)),
            pltpu.SemaphoreType.DMA((2, 2)),
            pltpu.SemaphoreType.DMA((2, 2)),
            pltpu.SemaphoreType.DMA((2, 2)),
        ],
        compiler_params=pltpu.CompilerParams(
            collective_id=0, has_side_effects=True, vmem_limit_bytes=48 * 1024 * 1024
        ),
    )(
        jnp.transpose(tracers, (1, 0, 2)),
        courant,
        switches,
        day_flags,
        diffusion_counts,
        night_rates,
        photo_rates,
        level_light[None],
        self_loss[None],
        vertical_mixing[None],
    )
    return jnp.transpose(out, (1, 0, 2))


def solution(mesh):
    grid = P(None, "lat", "lon")
    plane = P("lat", "lon")
    in_specs = (grid, grid, grid, plane, plane, P(), P(), P(), P(), P())
    return jax.shard_map(shards, mesh=mesh, in_specs=in_specs, out_specs=grid, check_vma=False)
```
